256 devices in a mesh: seg: 2 (over y_lo), chan: 128 (over x, y_hi, z, core).
Axes of the slice: x: 4, y: 4 (y_hi: 2, y_lo: 2; y = y_hi * 2 + y_lo), z: 8, core: 2. Of those that a mesh axis runs over, the one named last changes fastest.
Arguments:
- traces: bfloat16 [2, 8192, 4096], P('seg', 'chan'), may hold values from -60 to 60
- partners: int32 [128, 11], P('chan'), may hold values from -1 to 127, as said below
Outputs:
- stacked: float32 [128, 11, 65, 4096], P('chan', None, None, 'seg')
The draws below stay inside these ranges and needn't reach their ends.
Inputs may be any that keep to these rules, and one draw needn't show every extreme that they name: `partners`: entry q of block i is i + q - 5 if blocks i and i + q - 5 form a pair and -1 otherwise. Entry 5 is always i. The list is symmetric: j stands in the row of i exactly when i stands in the row of j.
All inputs are finite; a program needn't handle non-finite values.
Results may differ from the reference program's by a relative error of at most 0.013.
Values may be sent and summed in bfloat16 or wider, within the bound.
A program may use at most 128 MiB of HBM per device.

```python
import math
import jax
import jax.numpy as jnp
from jax import lax

CHB = 64
SAMPLES = 4096
BAND = 256
BAND_LO = 16
REACH = 5
LAGS = 65
CAP = 11
NB = 128
NCH = 8192
NSEG = 2


def draw_traces(key, part):
    key_scale, key_base = jax.random.split(key, 2)
    amplitude = jnp.exp(jax.random.uniform(key_scale, (NSEG, NCH, 1), jnp.float32, 0.0, math.log(10.0)))
    signal = jnp.clip(jax.random.normal(key_base, (NSEG, NCH, SAMPLES), jnp.float32), -6.0, 6.0)
    return (signal * amplitude).astype(jnp.bfloat16)


def draw_partners(key, part):
    keeps = jax.random.randint(key, (NB, REACH), 0, 10, dtype=jnp.int32) < 7
    blocks = jnp.arange(NB, dtype=jnp.int32)
    entries = []
    for slot in range(2 * REACH + 1):
        offset = slot - REACH
        if offset == 0:
            entries.append(blocks)
        elif offset < 0:
            distance = -offset
            kept = jnp.roll(keeps[:, distance - 1], distance)
            live = kept & (blocks >= distance)
            entries.append(jnp.where(live, blocks + offset, -1))
        else:
            live = keeps[:, offset - 1] & (blocks + offset < NB)
            entries.append(jnp.where(live, blocks + offset, -1))
    return jnp.stack(entries, axis=1).astype(jnp.int32)


def setup_inputs(seed: int = 0) -> dict:
    streams_of = jax.random.split(jax.random.key(seed), 3)
    traces = draw_traces(jax.random.fold_in(streams_of[2], 71), 0)
    partners = draw_partners(jax.random.fold_in(streams_of[2], 71), 0)
    return dict(traces=traces, partners=partners)


full_turn = 2.0 * math.pi
water_level = 0.5
epsilon = 1e-06

def lag_tables(band_bins, band_low, lag_count, samples):
    lag_half = (lag_count - 1) // 2
    bins = jnp.arange(band_bins, dtype=jnp.int32) + band_low
    shifts = jnp.arange(lag_count, dtype=jnp.int32) - lag_half
    phase = jnp.mod(shifts[:, None] * bins[None, :], samples)
    angle = phase.astype(jnp.float32) * (full_turn / samples)
    return (jnp.cos(angle), jnp.sin(angle))

def whiten(real_part, imag_part):
    power = real_part * real_part + imag_part * imag_part
    level = lax.optimization_barrier(jnp.mean(power, axis=-1, keepdims=True))
    denom = jnp.sqrt(power + water_level * level + epsilon)
    return jnp.concatenate([real_part / denom, imag_part / denom], axis=-1).astype(jnp.bfloat16)

def lagged(spectra, cos_table, sin_table):
    band_bins = cos_table.shape[1]
    lag_count = cos_table.shape[0]
    real_part = spectra[..., :band_bins].astype(jnp.float32)[None]
    imag_part = spectra[..., band_bins:].astype(jnp.float32)[None]
    cosine = cos_table[:, None, None, :]
    sine = sin_table[:, None, None, :]
    turned = jnp.concatenate([real_part * cosine - imag_part * sine, real_part * sine + imag_part * cosine], axis=-1)
    return turned.reshape(lag_count * spectra.shape[0], spectra.shape[1] * 2 * band_bins).astype(jnp.bfloat16)

def columns(window):
    moved = jnp.transpose(window, (0, 3, 1, 2))
    return moved.reshape(window.shape[0] * window.shape[3], window.shape[1] * window.shape[2])

def tile_block(lagged_rows, partner_columns, live_pairs, rows_a, norm_scale):
    product = jnp.dot(lagged_rows, partner_columns, preferred_element_type=jnp.float32)
    slots = live_pairs.shape[0]
    lag_count = product.shape[0] // rows_a
    width = product.shape[1] // slots
    product = product.reshape(lag_count, rows_a, slots, width).transpose(2, 0, 1, 3)
    product = product.reshape(slots, lag_count, rows_a * width)
    return product * norm_scale * live_pairs[:, None, None]

def reference(traces, partners):
    signal = traces.astype(jnp.float32)
    spectrum = jnp.fft.rfft(signal, axis=-1)[..., BAND_LO:BAND_LO + BAND]
    white = whiten(jnp.real(spectrum), jnp.imag(spectrum))
    blocks = white.reshape(NSEG, NB, CHB, 2 * BAND)
    padded = jnp.pad(blocks, ((0, 0), (REACH, REACH), (0, 0), (0, 0)))
    cos_table, sin_table = lag_tables(BAND, BAND_LO, LAGS, SAMPLES)
    norm_scale = (NSEG * BAND) ** (-0.5)

    def one_block(index):
        window = lax.dynamic_slice_in_dim(padded, index, CAP, 1)
        own_block = lax.dynamic_slice_in_dim(blocks, index, 1, 1)[:, 0]
        rows = lagged(jnp.transpose(own_block, (1, 0, 2)), cos_table, sin_table)
        pair_row = lax.dynamic_index_in_dim(partners, index, 0, keepdims=False)
        live_pairs = (pair_row >= 0).astype(jnp.float32)
        return tile_block(rows, columns(window), live_pairs, CHB, norm_scale)
    return lax.map(one_block, jnp.arange(NB, dtype=jnp.int32))
```

```python
import functools
import math

import jax
import jax.numpy as jnp
import numpy as np
from jax import lax
from jax.experimental import pallas as pl
from jax.experimental.pallas import tpu as pltpu
from jax.sharding import PartitionSpec as P

CHB = 64
SAMPLES = 4096
BAND = 256
BAND_LO = 16
LAGS = 65
CAP = 11
COLS = 256
FOLDS = SAMPLES // COLS
PLACES = 12
IN_FIRST = 8
FULL_TURN = 2.0 * math.pi
WATER_LEVEL = 0.5
EPSILON = 1e-06
HALF = 32
PAIRS = HALF // 2
CHUNK = 13
QUARTER = SAMPLES // 4


def tables():
    bins = np.arange(BAND, dtype=np.int64) + BAND_LO
    fine = (np.arange(COLS, dtype=np.int64)[:, None] * bins[None, :]) % SAMPLES
    angle = fine * (FULL_TURN / SAMPLES)
    transform = np.concatenate([np.cos(angle), -np.sin(angle)], axis=1).astype(np.float32)
    high = transform.astype(jnp.bfloat16)
    low = (transform - high.astype(np.float32)).astype(jnp.bfloat16)
    coarse = (COLS * np.arange(FOLDS, dtype=np.int64)[:, None] * bins[None, :]) % SAMPLES
    turn = coarse * (FULL_TURN / SAMPLES)
    twiddle = np.stack([np.cos(turn), np.sin(turn)]).astype(np.float32)
    shifts = np.arange(LAGS, dtype=np.int64) - (LAGS - 1) // 2
    phase = ((shifts[:, None] * bins[None, :]) % SAMPLES) * (FULL_TURN / SAMPLES)
    turns = np.stack([np.cos(phase), np.sin(phase)]).astype(np.float32)
    return np.stack([high, low]), twiddle, turns


def spectra(samples, ready, transform, twiddle):
    real = imag = None
    for group in range(4):
        ready(group)
        part = jnp.concatenate(
            [samples[:, (group * 4 + inner) * COLS : (group * 4 + inner + 1) * COLS] for inner in range(4)], axis=0
        )
        partial = jnp.dot(part, transform[0], preferred_element_type=jnp.float32)
        partial = partial + jnp.dot(part, transform[1], preferred_element_type=jnp.float32)
        for inner in range(4):
            fold = group * 4 + inner
            re = partial[inner * CHB : (inner + 1) * CHB, :BAND]
            im = partial[inner * CHB : (inner + 1) * CHB, BAND:]
            if fold == 0:
                real, imag = re, im
            else:
                cosine = twiddle[0, pl.ds(fold, 1), :]
                sine = twiddle[1, pl.ds(fold, 1), :]
                real = real + (re * cosine + im * sine)
                imag = imag + (im * cosine - re * sine)
    power = real * real + imag * imag
    level = jnp.sum(power, axis=-1, keepdims=True) * (1.0 / BAND)
    denom = jnp.sqrt(power + WATER_LEVEL * level + EPSILON)
    return jnp.concatenate([real / denom, imag / denom], axis=-1).astype(jnp.bfloat16)


def lag_rows(white, rows, turns, rotated, segment):
    for part in range(4):
        rows[part] = white[:, part * 128 : (part + 1) * 128].astype(jnp.float32)
    split = jnp.concatenate(
        [
            jnp.concatenate([rows[part, pl.ds(odd, PAIRS, stride=2), :] for part in range(4)], axis=1)
            for odd in range(2)
        ],
        axis=0,
    )
    re, im = split[:, :BAND], split[:, BAND:]

    @pl.loop(0, LAGS // 5)
    def _(step):
        for inner in range(5):
            lag = step * 5 + inner
            cosine = turns[0, pl.ds(lag, 1), :]
            sine = turns[1, pl.ds(lag, 1), :]
            at = pl.ds(pl.multiple_of(lag * HALF, HALF), HALF)
            rotated[segment, at, :BAND] = (re * cosine - im * sine).astype(jnp.bfloat16)
            rotated[segment, at, BAND:] = (re * sine + im * cosine).astype(jnp.bfloat16)


def correlate(rotated, window, first, count, scale_of, store):
    right = jnp.concatenate(
        [window[seg, first : first + count].reshape(count * CHB, 2 * BAND) for seg in range(2)], axis=1
    )
    lane = lax.broadcasted_iota(jnp.int32, (PAIRS, 2 * CHB), 1)
    low_half = lane < CHB
    scales = [scale_of(first + k) for k in range(count)]

    @pl.loop(0, LAGS // CHUNK)
    def _(chunk):
        at = pl.ds(pl.multiple_of(chunk * CHUNK * HALF, HALF), CHUNK * HALF)
        left = jnp.concatenate([rotated[0, at, :], rotated[1, at, :]], axis=1)
        product = lax.dot_general(
            left, right, (((1,), (1,)), ((), ())), preferred_element_type=jnp.float32
        )
        for inner in range(CHUNK):
            lag = chunk * CHUNK + inner
            for k in range(0, count, 2):
                width = min(2, count - k) * CHB
                even = product[inner * HALF : inner * HALF + PAIRS, k * CHB : k * CHB + width]
                odd = product[inner * HALF + PAIRS : (inner + 1) * HALF, k * CHB : k * CHB + width]
                if width < 2 * CHB:
                    store(first + k, lag, jnp.concatenate([even, odd], axis=1) * scales[k])
                else:
                    here = jnp.where(low_half, even, pltpu.roll(odd, CHB, 1))
                    there = jnp.where(low_half, pltpu.roll(even, CHB, 1), odd)
                    store(first + k, lag, here * scales[k])
                    store(first + k + 1, lag, there * scales[k + 1])


def slot_of(place, core):
    if isinstance(place, int) and place == 1:
        return 10 * core
    return place - 1 - core


def gather_kernel(
    traces, transform_in, twiddle_in, turns_in, partners,
    window, rotated, done,
    samples, transform, twiddle, turns, rows, in_sem, send_sem, recv_sem,
):
    seg = lax.axis_index("seg")
    chan = lax.axis_index("chan")
    core = chan % 2
    spot = (chan // 2) % 8
    other = 1 - seg
    total = lax.axis_size("chan")

    loads = [
        pltpu.make_async_copy(
            traces.at[0, :, pl.ds(part * QUARTER, QUARTER)],
            samples.at[:, pl.ds(part * QUARTER, QUARTER)],
            in_sem.at[part],
        )
        for part in range(4)
    ]
    tables_in = [
        pltpu.make_async_copy(transform_in, transform, in_sem.at[4]),
        pltpu.make_async_copy(twiddle_in, twiddle, in_sem.at[5]),
    ]
    turns_load = pltpu.make_async_copy(turns_in, turns, in_sem.at[6])
    for load in tables_in + loads + [turns_load]:
        load.start()

    def segment_at(distance):
        crossed = (spot + distance < 0) | (spot + distance > 7)
        return jnp.where(crossed, other, seg)

    after = {"seg": segment_at(1), "chan": (chan + 2) % total}
    before = {"seg": segment_at(-1), "chan": (chan + total - 2) % total}
    rung = {"seg": other, "chan": chan}
    sibling = {"seg": seg, "chan": chan + 1 - 2 * core}
    diagonal = {
        "seg": jnp.where(core == 1, segment_at(1), segment_at(-1)),
        "chan": (chan + total - 1 + 2 * core) % total,
    }

    barrier = pltpu.get_barrier_semaphore()
    for device in (after, before, rung, sibling, diagonal):
        pl.semaphore_signal(barrier, inc=1, device_id=device, device_id_type=pl.DeviceIdType.MESH)

    sends = []

    def send(label, source, target, device):
        copy = pltpu.make_async_remote_copy(
            src_ref=window.at[label, source],
            dst_ref=window.at[label, target],
            send_sem=send_sem.at[len(sends)],
            recv_sem=recv_sem.at[label, target],
            device_id=device,
            device_id_type=pl.DeviceIdType.MESH,
        )
        copy.start()
        sends.append(copy)

    def arrived(label, place):
        pltpu.make_async_remote_copy(
            src_ref=window.at[label, place],
            dst_ref=window.at[label, place],
            send_sem=send_sem.at[0],
            recv_sem=recv_sem.at[label, place],
            device_id=rung,
            device_id_type=pl.DeviceIdType.MESH,
        ).wait_recv()

    for load in tables_in:
        load.wait()
    mine = 6 + core
    window[seg, mine] = spectra(samples, lambda part: loads[part].wait(), transform, twiddle)

    pl.semaphore_wait(barrier, 5)
    send(seg, mine, mine, rung)
    send(seg, mine, 4 + core, after)
    send(seg, mine, 8 + core, before)
    send(seg, mine, mine, sibling)

    turns_load.wait()
    own = pl.ds(pl.multiple_of(seg * HALF, HALF), HALF)
    lag_rows(window[seg, mine, own, :], rows, turns, rotated, seg)

    arrived(other, mine)
    send(other, mine, 4 + core, after)
    send(other, mine, 8 + core, before)
    send(other, mine, mine, sibling)
    lag_rows(window[other, mine, own, :], rows, turns, rotated, other)

    for turn in range(2):
        for distance, target, device in ((-1, 2, after), (1, 10, before)):
            label = segment_at(distance)
            label = label if turn == 0 else 1 - label
            place = 6 + 2 * distance + core
            arrived(label, place)
            send(label, place, target + core, device)
            send(label, place, place, sibling)

    def live_scale(place):
        live = partners[0, slot_of(place, core)] >= 0
        return jnp.where(live, jnp.float32((2 * BAND) ** -0.5), jnp.float32(0.0))

    def store(place, lag, tile):
        done[place - 4, lag] = tile

    def from_sibling(*pairs):
        for pair in pairs:
            for label in range(2):
                arrived(label, pair + 1 - core)

    from_sibling(4, 6)
    correlate(rotated, window, 4, 4, live_scale, store)

    corner = len(sends)
    sends.extend([None, None])
    for turn in range(2):
        for distance in (-2, 2):
            label = segment_at(distance)
            label = label if turn == 0 else 1 - label
            place = 6 + 2 * distance + core
            arrived(label, place)

            @pl.when(core == (1 if distance < 0 else 0))
            def _():
                copy = pltpu.make_async_remote_copy(
                    src_ref=window.at[label, place],
                    dst_ref=window.at[label, 1],
                    send_sem=send_sem.at[corner + turn],
                    recv_sem=recv_sem.at[label, 1],
                    device_id=diagonal,
                    device_id_type=pl.DeviceIdType.MESH,
                )
                copy.start()

            send(label, place, place, sibling)

    from_sibling(8, 10)
    correlate(rotated, window, 8, 4, live_scale, store)

    from_sibling(2)
    for label in range(2):
        arrived(label, 1)
    for number, copy in enumerate(sends):
        if copy is None:
            copy = pltpu.make_async_remote_copy(
                src_ref=window.at[0, 1],
                dst_ref=window.at[0, 1],
                send_sem=send_sem.at[number],
                recv_sem=recv_sem.at[0, 1],
                device_id=diagonal,
                device_id_type=pl.DeviceIdType.MESH,
            )
        copy.wait_send()


def finish_kernel(window, rotated, done, partners, out, last, out_sem):
    core = lax.axis_index("chan") % 2
    copies = []
    for k in range(IN_FIRST):
        copies.append(pltpu.make_async_copy(done.at[k], out.at[slot_of(4 + k, core)], out_sem.at[k]))
        copies[-1].start()

    def live_scale(place):
        live = partners[0, slot_of(place, core)] >= 0
        return jnp.where(live, jnp.float32((2 * BAND) ** -0.5), jnp.float32(0.0))

    def store(place, lag, tile):
        last[place - 1, lag] = tile

    correlate(rotated, window, 1, 3, live_scale, store)
    for k in range(3):
        copies.append(
            pltpu.make_async_copy(last.at[k], out.at[slot_of(1 + k, core)], out_sem.at[IN_FIRST + k])
        )
        copies[-1].start()
    for copy in copies:
        copy.wait()


def local(traces, partners):
    transform, twiddle, turns = tables()
    in_hbm = pl.BlockSpec(memory_space=pltpu.HBM)
    in_vmem = pl.BlockSpec(memory_space=pltpu.VMEM)
    in_smem = pl.BlockSpec(memory_space=pltpu.SMEM)
    window, rotated, done = pl.pallas_call(
        gather_kernel,
        out_shape=(
            pltpu.VMEM((2, PLACES, CHB, 2 * BAND), jnp.bfloat16),
            pltpu.VMEM((2, LAGS * HALF, 2 * BAND), jnp.bfloat16),
            pltpu.VMEM((IN_FIRST, LAGS, PAIRS, 2 * CHB), jnp.float32),
        ),
        in_specs=[in_hbm] * 4 + [in_smem],
        out_specs=(in_vmem,) * 3,
        scratch_shapes=[
            pltpu.VMEM((CHB, SAMPLES), jnp.bfloat16),
            pltpu.VMEM((2, COLS, 2 * BAND), jnp.bfloat16),
            pltpu.VMEM((2, FOLDS, BAND), jnp.float32),
            pltpu.VMEM((2, LAGS, BAND), jnp.float32),
            pltpu.VMEM((4, HALF, 128), jnp.float32),
            pltpu.SemaphoreType.DMA((7,)),
            pltpu.SemaphoreType.DMA((32,)),
            pltpu.SemaphoreType.DMA((2, PLACES)),
        ],
        compiler_params=pltpu.CompilerParams(
            collective_id=0, has_side_effects=True, vmem_limit_bytes=40 * 2**20
        ),
        name="gather",
    )(*[pltpu.with_memory_space_constraint(jnp.asarray(x), pltpu.HBM) for x in (traces, transform, twiddle, turns)], partners)
    out = pl.pallas_call(
        finish_kernel,
        out_shape=jax.ShapeDtypeStruct((CAP, LAGS, PAIRS, 2 * CHB), jnp.float32),
        in_specs=[in_vmem] * 3 + [in_smem],
        out_specs=in_hbm,
        scratch_shapes=[
            pltpu.VMEM((3, LAGS, PAIRS, 2 * CHB), jnp.float32),
            pltpu.SemaphoreType.DMA((CAP,)),
        ],
        compiler_params=pltpu.CompilerParams(vmem_limit_bytes=40 * 2**20),
        name="finish",
    )(window, rotated, done, partners)
    return out.reshape(1, CAP, LAGS, HALF * CHB)


def solution(mesh):
    placed = (P("seg", "chan", None), P("chan", None))
    return jax.shard_map(
        local, mesh=mesh, in_specs=placed, out_specs=P("chan", None, None, "seg"), check_vma=False
    )
```

```python
import functools
import math

import jax
import jax.numpy as jnp
import numpy as np
from jax import lax
from jax.experimental import pallas as pl
from jax.experimental.pallas import tpu as pltpu
from jax.sharding import PartitionSpec as P

CHB = 64
SAMPLES = 4096
BAND = 256
BAND_LO = 16
LAGS = 65
CAP = 11
COLS = 256
FOLDS = SAMPLES // COLS
PLACES = 12
IN_FIRST = 8
FULL_TURN = 2.0 * math.pi
WATER_LEVEL = 0.5
EPSILON = 1e-06
HALF = 32
PAIRS = HALF // 2
EARLY = True
QUARTER = SAMPLES // 4


def tables():
    bins = np.arange(BAND, dtype=np.int64) + BAND_LO
    fine = (np.arange(COLS, dtype=np.int64)[:, None] * bins[None, :]) % SAMPLES
    angle = fine * (FULL_TURN / SAMPLES)
    transform = np.concatenate([np.cos(angle), -np.sin(angle)], axis=1).astype(np.float32)
    high = transform.astype(jnp.bfloat16)
    low = (transform - high.astype(np.float32)).astype(jnp.bfloat16)
    coarse = (COLS * np.arange(FOLDS, dtype=np.int64)[:, None] * bins[None, :]) % SAMPLES
    turn = coarse * (FULL_TURN / SAMPLES)
    twiddle = np.stack([np.cos(turn), np.sin(turn)]).astype(np.float32)
    shifts = np.arange(LAGS, dtype=np.int64) - (LAGS - 1) // 2
    phase = ((shifts[:, None] * bins[None, :]) % SAMPLES) * (FULL_TURN / SAMPLES)
    turns = np.stack([np.cos(phase), np.sin(phase)]).astype(np.float32)
    return np.stack([high, low]), twiddle, turns


def spectra(samples, ready, transform, twiddle):
    real = imag = None
    for group in range(4):
        ready(group)
        part = jnp.concatenate(
            [samples[:, (group * 4 + inner) * COLS : (group * 4 + inner + 1) * COLS] for inner in range(4)], axis=0
        )
        partial = jnp.dot(part, transform[0], preferred_element_type=jnp.float32)
        partial = partial + jnp.dot(part, transform[1], preferred_element_type=jnp.float32)
        for inner in range(4):
            fold = group * 4 + inner
            re = partial[inner * CHB : (inner + 1) * CHB, :BAND]
            im = partial[inner * CHB : (inner + 1) * CHB, BAND:]
            if fold == 0:
                real, imag = re, im
            else:
                cosine = twiddle[0, pl.ds(fold, 1), :]
                sine = twiddle[1, pl.ds(fold, 1), :]
                real = real + (re * cosine + im * sine)
                imag = imag + (im * cosine - re * sine)
    power = real * real + imag * imag
    level = jnp.sum(power, axis=-1, keepdims=True) * (1.0 / BAND)
    denom = jnp.sqrt(power + WATER_LEVEL * level + EPSILON)
    return jnp.concatenate([real / denom, imag / denom], axis=-1).astype(jnp.bfloat16)


def lag_rows(white, rows, turns, rotated, segment):
    for part in range(4):
        rows[part] = white[:, part * 128 : (part + 1) * 128].astype(jnp.float32)
    split = jnp.concatenate(
        [
            jnp.concatenate([rows[part, pl.ds(odd, PAIRS, stride=2), :] for part in range(4)], axis=1)
            for odd in range(2)
        ],
        axis=0,
    )
    re, im = split[:, :BAND], split[:, BAND:]

    @pl.loop(0, LAGS // 5)
    def _(step):
        for inner in range(5):
            lag = step * 5 + inner
            cosine = turns[0, pl.ds(lag, 1), :]
            sine = turns[1, pl.ds(lag, 1), :]
            at = pl.ds(pl.multiple_of(lag * HALF, HALF), HALF)
            rotated[segment, at, :BAND] = (re * cosine - im * sine).astype(jnp.bfloat16)
            rotated[segment, at, BAND:] = (re * sine + im * cosine).astype(jnp.bfloat16)


def correlate(rotated, window, first, count, scale_of, store):
    right = jnp.concatenate(
        [window[seg, first : first + count].reshape(count * CHB, 2 * BAND) for seg in range(2)], axis=1
    )
    left = jnp.concatenate([rotated[0], rotated[1]], axis=1)
    product = lax.dot_general(left, right, (((1,), (1,)), ((), ())), preferred_element_type=jnp.float32)
    product = product.reshape(LAGS, 2, PAIRS, count * CHB)
    low_half = lax.broadcasted_iota(jnp.int32, (LAGS, PAIRS, 2 * CHB), 2) < CHB
    for k in range(0, count, 2):
        width = min(2, count - k) * CHB
        even = product[:, 0, :, k * CHB : k * CHB + width]
        odd = product[:, 1, :, k * CHB : k * CHB + width]
        if width < 2 * CHB:
            store(first + k, jnp.concatenate([even, odd], axis=2) * scale_of(first + k))
        else:
            here = jnp.where(low_half, even, pltpu.roll(odd, CHB, 2))
            there = jnp.where(low_half, pltpu.roll(even, CHB, 2), odd)
            store(first + k, here * scale_of(first + k))
            store(first + k + 1, there * scale_of(first + k + 1))


def slot_of(place, core):
    if isinstance(place, int) and place == 1:
        return 10 * core
    return place - 1 - core


def gather_kernel(
    traces, transform_in, twiddle_in, turns_in, partners_in,
    window, rotated, done, last_scales,
    samples, transform, twiddle, turns, rows, partners, in_sem, send_sem, recv_sem,
):
    seg = lax.axis_index("seg")
    chan = lax.axis_index("chan")
    core = chan % 2
    chip = chan // 2
    spot = chip % 8
    other = 1 - seg
    total = lax.axis_size("chan")
    chips = total // 2
    mine = 6 + core

    tables_in = [
        pltpu.make_async_copy(transform_in, transform, in_sem.at[4]),
        pltpu.make_async_copy(twiddle_in, twiddle, in_sem.at[5]),
    ]
    loads = [
        pltpu.make_async_copy(
            traces.at[0, :, pl.ds(part * QUARTER, QUARTER)],
            samples.at[:, pl.ds(part * QUARTER, QUARTER)],
            in_sem.at[part],
        )
        for part in range(4)
    ]
    later = [
        pltpu.make_async_copy(turns_in, turns, in_sem.at[6]),
        pltpu.make_async_copy(partners_in, partners, in_sem.at[7]),
    ]
    for load in tables_in + loads + later:
        load.start()

    def there_is(distance):
        return (chip + distance >= 0) & (chip + distance < chips)

    def segment_at(distance):
        crossed = (spot + distance < 0) | (spot + distance > 7)
        return jnp.where(crossed, other, seg)

    def along(distance, cross=False):
        label = segment_at(distance)
        return {"seg": 1 - label if cross else label, "chan": (chan + total + 2 * distance) % total}

    near = jnp.where(spot == 0, 1, -1)
    outward = 2 * core - 1
    rung = {"seg": other, "chan": chan}
    sibling = {"seg": seg, "chan": chan + 1 - 2 * core}
    corner = {"seg": segment_at(2 * outward), "chan": (chan + total + 3 * outward) % total}

    barrier = pltpu.get_barrier_semaphore()

    def greet(device):
        pl.semaphore_signal(barrier, inc=1, device_id=device, device_id_type=pl.DeviceIdType.MESH)

    greet(rung)
    greet(sibling)
    greeted = jnp.int32(2)
    for distance in (1, -1):

        @pl.when(there_is(distance))
        def _():
            greet(along(distance))
            greet(along(distance, True))

        greeted = greeted + jnp.where(there_is(distance), 2, 0)

    @pl.when(there_is(2 * outward))
    def _():
        greet(corner)

    greeted = greeted + jnp.where(there_is(2 * outward), 1, 0)

    sends = []

    def send(label, source, target, device, valid=None):
        copy = pltpu.make_async_remote_copy(
            src_ref=window.at[label, source],
            dst_ref=window.at[label, target],
            send_sem=send_sem.at[len(sends)],
            recv_sem=recv_sem.at[label, target],
            device_id=device,
            device_id_type=pl.DeviceIdType.MESH,
        )
        sends.append((copy, valid))
        if valid is None:
            copy.start()
        else:
            pl.when(valid)(copy.start)

    def arrived(label, place):
        pltpu.make_async_remote_copy(
            src_ref=window.at[label, place],
            dst_ref=window.at[label, place],
            send_sem=send_sem.at[0],
            recv_sem=recv_sem.at[label, place],
            device_id=rung,
            device_id_type=pl.DeviceIdType.MESH,
        ).wait_recv()

    for load in tables_in:
        load.wait()
    window[seg, mine] = spectra(samples, lambda part: loads[part].wait(), transform, twiddle)

    pl.semaphore_wait(barrier, greeted)
    for cross in (False, True):
        for distance in (-near, near):
            send(seg, mine, 6 - 2 * distance + core, along(distance, cross), there_is(distance))
    send(seg, mine, mine, rung)
    send(seg, mine, mine, sibling)

    for distance in (-2, -1, 1, 2):

        @pl.when(jnp.logical_not(there_is(distance)))
        def _():
            window[:, 6 + 2 * distance : 8 + 2 * distance] = jnp.zeros((2, 2, CHB, 2 * BAND), jnp.bfloat16)

    lone = there_is(3 * outward)

    @pl.when(jnp.logical_not(lone))
    def _():
        window[:, 1] = jnp.zeros((2, CHB, 2 * BAND), jnp.bfloat16)

    for load in later:
        load.wait()
    own = pl.ds(pl.multiple_of(seg * HALF, HALF), HALF)
    lag_rows(window[seg, mine, own, :], rows, turns, rotated, seg)

    def from_neighbour(distance, turn):
        label = segment_at(distance)
        label = label if turn == 0 else 1 - label
        place = 6 + 2 * distance + core
        pl.when(there_is(distance))(lambda: arrived(label, place))
        return label, place

    for turn in range(2):
        for distance in (near, -near):
            label, place = from_neighbour(distance, turn)
            here = there_is(distance)
            if turn == 0:
                send(label, place, 1, corner, here & there_is(-2 * distance) & (distance == -outward))
            send(label, place, 6 + 4 * distance + core, along(-distance), here & there_is(-distance))
            send(label, place, place, sibling, here)
        if turn == 0:
            arrived(other, mine)
            send(other, mine, mine, sibling)
            lag_rows(window[other, mine, own, :], rows, turns, rotated, other)

    def live_scale(place):
        live = partners[0, slot_of(place, core)] >= 0
        return jnp.where(live, jnp.float32((2 * BAND) ** -0.5), jnp.float32(0.0))

    def store(place, tile):
        done[place - 4] = tile

    def from_sibling(*distances):
        for distance in distances:

            @pl.when(there_is(distance))
            def _():
                for label in range(2):
                    arrived(label, 7 + 2 * distance - core)

    for place in range(1, 4):
        last_scales[place - 1] = jnp.full((8, 2 * CHB), live_scale(place), jnp.float32)

    from_sibling(0)
    if EARLY:
        from_sibling(-1)
        correlate(rotated, window, 4, 4, live_scale, store)
    for distance in (2 * near, -2 * near):
        label, place = from_neighbour(distance, 0)
        send(label, place, place, sibling, there_is(distance))
    across = segment_at(3 * outward)
    pl.when(lone)(lambda: arrived(across, 1))
    send(across, 1, 1, rung, lone)
    for distance in (2 * near, -2 * near):
        label, place = from_neighbour(distance, 1)
        send(label, place, place, sibling, there_is(distance))
    if not EARLY:
        from_sibling(-1)
        correlate(rotated, window, 4, 4, live_scale, store)
    from_sibling(1, 2)
    correlate(rotated, window, 8, 4, live_scale, store)

    from_sibling(-2)
    pl.when(lone)(lambda: arrived(1 - across, 1))
    for copy, valid in sends:
        if valid is None:
            copy.wait_send()
        else:
            pl.when(valid)(copy.wait_send)


def finish_kernel(window, rotated, done, last_scales, out, last, out_sem):
    core = lax.axis_index("chan") % 2
    copies = []
    for k in range(IN_FIRST):
        copies.append(pltpu.make_async_copy(done.at[k], out.at[slot_of(4 + k, core)], out_sem.at[k]))
        copies[-1].start()

    def scale(place):
        return last_scales[place - 1, 0:1, :].reshape(1, 1, 2 * CHB)

    def store(place, tile):
        last[place - 1] = tile

    correlate(rotated, window, 1, 3, scale, store)
    for k in range(3):
        copies.append(
            pltpu.make_async_copy(last.at[k], out.at[slot_of(1 + k, core)], out_sem.at[IN_FIRST + k])
        )
        copies[-1].start()
    for copy in copies:
        copy.wait()


def local(traces, partners):
    transform, twiddle, turns = tables()
    in_hbm = pl.BlockSpec(memory_space=pltpu.HBM)
    in_vmem = pl.BlockSpec(memory_space=pltpu.VMEM)
    operands = [
        pltpu.with_memory_space_constraint(jnp.asarray(x), pltpu.HBM)
        for x in (traces, transform, twiddle, turns, partners)
    ]
    results = pl.pallas_call(
        gather_kernel,
        out_shape=(
            pltpu.VMEM((2, PLACES, CHB, 2 * BAND), jnp.bfloat16),
            pltpu.VMEM((2, LAGS * HALF, 2 * BAND), jnp.bfloat16),
            pltpu.VMEM((IN_FIRST, LAGS, PAIRS, 2 * CHB), jnp.float32),
            pltpu.VMEM((3, 8, 2 * CHB), jnp.float32),
        ),
        in_specs=[in_hbm] * 5,
        out_specs=(in_vmem,) * 4,
        scratch_shapes=[
            pltpu.VMEM((CHB, SAMPLES), jnp.bfloat16),
            pltpu.VMEM((2, COLS, 2 * BAND), jnp.bfloat16),
            pltpu.VMEM((2, FOLDS, BAND), jnp.float32),
            pltpu.VMEM((2, LAGS, BAND), jnp.float32),
            pltpu.VMEM((4, HALF, 128), jnp.float32),
            pltpu.SMEM((1, CAP), jnp.int32),
            pltpu.SemaphoreType.DMA((8,)),
            pltpu.SemaphoreType.DMA((32,)),
            pltpu.SemaphoreType.DMA((2, PLACES)),
        ],
        compiler_params=pltpu.CompilerParams(
            collective_id=0, has_side_effects=True, vmem_limit_bytes=40 * 2**20
        ),
        name="gather",
    )(*operands)
    out = pl.pallas_call(
        finish_kernel,
        out_shape=jax.ShapeDtypeStruct((CAP, LAGS, PAIRS, 2 * CHB), jnp.float32),
        in_specs=[in_vmem] * 4,
        out_specs=in_hbm,
        scratch_shapes=[
            pltpu.VMEM((3, LAGS, PAIRS, 2 * CHB), jnp.float32),
            pltpu.SemaphoreType.DMA((CAP,)),
        ],
        compiler_params=pltpu.CompilerParams(vmem_limit_bytes=40 * 2**20),
        name="finish",
    )(*results)
    return out.reshape(1, CAP, LAGS, HALF * CHB)


def solution(mesh):
    placed = (P("seg", "chan", None), P("chan", None))
    return jax.shard_map(
        local, mesh=mesh, in_specs=placed, out_specs=P("chan", None, None, "seg"), check_vma=False
    )
```

```python
import functools
import math

import jax
import jax.numpy as jnp
import numpy as np
from jax import lax
from jax.experimental import pallas as pl
from jax.experimental.pallas import tpu as pltpu
from jax.sharding import PartitionSpec as P

CHB = 64
SAMPLES = 4096
BAND = 256
BAND_LO = 16
LAGS = 65
CAP = 11
COLS = 256
FOLDS = SAMPLES // COLS
PLACES = 12
IN_FIRST = 8
FULL_TURN = 2.0 * math.pi
WATER_LEVEL = 0.5
EPSILON = 1e-06
HALF = 32
PAIRS = HALF // 2
PARTS = ((0, 22), (22, 44), (44, 65))


def tables():
    bins = np.arange(BAND, dtype=np.int64) + BAND_LO
    fine = (np.arange(COLS, dtype=np.int64)[:, None] * bins[None, :]) % SAMPLES
    angle = fine * (FULL_TURN / SAMPLES)
    transform = np.concatenate([np.cos(angle), -np.sin(angle)], axis=1).astype(np.float32)
    high = transform.astype(jnp.bfloat16)
    low = (transform - high.astype(np.float32)).astype(jnp.bfloat16)
    coarse = (COLS * np.arange(FOLDS, dtype=np.int64)[:, None] * bins[None, :]) % SAMPLES
    turn = coarse * (FULL_TURN / SAMPLES)
    twiddle = np.stack([np.cos(turn), np.sin(turn)]).astype(np.float32)
    shifts = np.arange(LAGS, dtype=np.int64) - (LAGS - 1) // 2
    phase = ((shifts[:, None] * bins[None, :]) % SAMPLES) * (FULL_TURN / SAMPLES)
    turns = np.stack([np.cos(phase), np.sin(phase)]).astype(np.float32)
    return np.stack([high, low]), twiddle, turns


def spectra(samples, transform, twiddle):
    count = samples.shape[0]
    part = jnp.concatenate([samples[:, fold * COLS : (fold + 1) * COLS] for fold in range(FOLDS)], axis=0)
    partial = jnp.dot(part, transform[0], preferred_element_type=jnp.float32)
    partial = partial + jnp.dot(part, transform[1], preferred_element_type=jnp.float32)
    real, imag = partial[:count, :BAND], partial[:count, BAND:]
    for fold in range(1, FOLDS):
        re = partial[fold * count : (fold + 1) * count, :BAND]
        im = partial[fold * count : (fold + 1) * count, BAND:]
        cosine = twiddle[0, pl.ds(fold, 1), :]
        sine = twiddle[1, pl.ds(fold, 1), :]
        real = real + (re * cosine + im * sine)
        imag = imag + (im * cosine - re * sine)
    power = real * real + imag * imag
    level = jnp.sum(power, axis=-1, keepdims=True) * (1.0 / BAND)
    denom = jnp.sqrt(power + WATER_LEVEL * level + EPSILON)
    return jnp.concatenate([real / denom, imag / denom], axis=-1).astype(jnp.bfloat16)


def lag_rows(white, rows, turns, rotated, segment):
    for part in range(4):
        rows[part] = white[:, part * 128 : (part + 1) * 128].astype(jnp.float32)
    split = jnp.concatenate(
        [
            jnp.concatenate([rows[part, pl.ds(odd, PAIRS, stride=2), :] for part in range(4)], axis=1)
            for odd in range(2)
        ],
        axis=0,
    )
    re, im = split[:, :BAND], split[:, BAND:]

    @pl.loop(0, LAGS // 5)
    def _(step):
        for inner in range(5):
            lag = step * 5 + inner
            cosine = turns[0, pl.ds(lag, 1), :]
            sine = turns[1, pl.ds(lag, 1), :]
            at = pl.ds(pl.multiple_of(lag * HALF, HALF), HALF)
            rotated[segment, at, :BAND] = (re * cosine - im * sine).astype(jnp.bfloat16)
            rotated[segment, at, BAND:] = (re * sine + im * cosine).astype(jnp.bfloat16)


def correlate(rotated, window, first, count, scale_of, store, parts=((0, LAGS),)):
    right = jnp.concatenate(
        [window[seg, first : first + count].reshape(count * CHB, 2 * BAND) for seg in range(2)], axis=1
    )
    for begin, end in parts:
        lags = end - begin
        left = jnp.concatenate([rotated[seg, begin * HALF : end * HALF, :] for seg in range(2)], axis=1)
        product = lax.dot_general(left, right, (((1,), (1,)), ((), ())), preferred_element_type=jnp.float32)
        product = product.reshape(lags, 2, PAIRS, count * CHB)
        low_half = lax.broadcasted_iota(jnp.int32, (lags, PAIRS, 2 * CHB), 2) < CHB
        for k in range(0, count, 2):
            width = min(2, count - k) * CHB
            even = product[:, 0, :, k * CHB : k * CHB + width]
            odd = product[:, 1, :, k * CHB : k * CHB + width]
            if width < 2 * CHB:
                store(first + k, begin, end, jnp.concatenate([even, odd], axis=2) * scale_of(first + k))
            else:
                here = jnp.where(low_half, even, pltpu.roll(odd, CHB, 2))
                there = jnp.where(low_half, pltpu.roll(even, CHB, 2), odd)
                store(first + k, begin, end, here * scale_of(first + k))
                store(first + k + 1, begin, end, there * scale_of(first + k + 1))


def slot_of(place, core):
    if isinstance(place, int) and place == 1:
        return 10 * core
    return place - 1 - core


def gather_kernel(
    traces, transform_in, twiddle_in, turns_in, partners_in,
    window, rotated, done, last_scales,
    samples, transform, twiddle, turns, rows, partners, in_sem, send_sem, recv_sem,
):
    seg = lax.axis_index("seg")
    chan = lax.axis_index("chan")
    core = chan % 2
    chip = chan // 2
    spot = chip % 8
    other = 1 - seg
    total = lax.axis_size("chan")
    chips = total // 2
    mine = 6 + core

    tables_in = [
        pltpu.make_async_copy(transform_in, transform, in_sem.at[4]),
        pltpu.make_async_copy(twiddle_in, twiddle, in_sem.at[5]),
    ]
    loads = [
        pltpu.make_async_copy(
            traces.at[0, pl.ds(half * HALF, HALF), :], samples.at[pl.ds(half * HALF, HALF), :], in_sem.at[half]
        )
        for half in range(2)
    ]
    later = [
        pltpu.make_async_copy(turns_in, turns, in_sem.at[6]),
        pltpu.make_async_copy(partners_in, partners, in_sem.at[7]),
    ]
    for load in tables_in + loads + later:
        load.start()

    def there_is(distance):
        return (chip + distance >= 0) & (chip + distance < chips)

    def segment_at(distance):
        crossed = (spot + distance < 0) | (spot + distance > 7)
        return jnp.where(crossed, other, seg)

    outward = 2 * core - 1
    exists = {distance: there_is(distance) for distance in (-2, -1, 1, 2)}
    exists[0] = None
    lone = there_is(3 * outward)
    reaches_corner = there_is(2 * outward)
    turns_corner = {distance: exists[distance] & reaches_corner & (outward == -distance) for distance in (-1, 1)}
    through = exists[1] & exists[-1]
    label_at = {distance: segment_at(distance) for distance in (-2, -1, 1, 2)}
    across = segment_at(3 * outward)

    def along(distance, cross=False):
        label = label_at[distance]
        return {"seg": 1 - label if cross else label, "chan": (chan + total + 2 * distance) % total}

    rung = {"seg": other, "chan": chan}
    sibling = {"seg": seg, "chan": chan + 1 - 2 * core}
    corner = {"seg": segment_at(2 * outward), "chan": (chan + total + 3 * outward) % total}

    def when(valid, act):
        if valid is None:
            act()
        else:
            pl.when(valid)(act)

    barrier = pltpu.get_barrier_semaphore()

    def greet(device):
        pl.semaphore_signal(barrier, inc=1, device_id=device, device_id_type=pl.DeviceIdType.MESH)

    greet(rung)
    greet(sibling)
    greeted = jnp.int32(2)
    for distance in (1, -1):

        @pl.when(exists[distance])
        def _():
            greet(along(distance))
            greet(along(distance, True))

        greeted = greeted + jnp.where(exists[distance], 2, 0)
    pl.when(reaches_corner)(lambda: greet(corner))
    greeted = greeted + jnp.where(reaches_corner, 1, 0)

    def send(key, label, source, target, device):
        both = label is None
        copy = pltpu.make_async_remote_copy(
            src_ref=window.at[:, source] if both else window.at[label, source],
            dst_ref=window.at[:, target] if both else window.at[label, target],
            send_sem=send_sem.at[key],
            recv_sem=recv_sem.at[2 if both else label, target],
            device_id=device,
            device_id_type=pl.DeviceIdType.MESH,
        )
        copy.start()

    def copy_of(number, blocks, place):
        return pltpu.make_async_remote_copy(
            src_ref=window.at[0, 0:blocks],
            dst_ref=window.at[0, 0:blocks],
            send_sem=send_sem.at[number],
            recv_sem=recv_sem.at[place],
            device_id=rung,
            device_id_type=pl.DeviceIdType.MESH,
        )

    def arrived(label, place):
        copy_of(0, 1, (label, place)).wait_recv()

    def own_to(distance, cross):
        send(distance % 4, seg, mine, 6 - 2 * distance + core, along(distance, cross))

    def own_out(cross):
        for distance in (1, -1):
            pl.when(exists[distance])(functools.partial(own_to, distance, cross))

    for load in tables_in + loads:
        load.wait()
    window[seg, mine] = spectra(samples[...], transform, twiddle)
    pl.semaphore_wait(barrier, greeted)
    own_out(False)
    own_out(True)
    send(0, seg, mine, mine, rung)

    for distance in (-2, -1, 1, 2):

        @pl.when(jnp.logical_not(exists[distance]))
        def _():
            window[:, 6 + 2 * distance : 8 + 2 * distance] = jnp.zeros((2, 2, CHB, 2 * BAND), jnp.bfloat16)

    @pl.when(jnp.logical_not(lone))
    def _():
        window[:, 1] = jnp.zeros((2, CHB, 2 * BAND), jnp.bfloat16)

    for load in later:
        load.wait()
    own = pl.ds(pl.multiple_of(seg * HALF, HALF), HALF)
    lag_rows(window[seg, mine, own, :], rows, turns, rotated, seg)

    arrived(other, mine)
    send(0, None, mine, mine, sibling)

    def pass_on(turn, *distances):
        for distance in distances:
            label = label_at[distance] if turn == 0 else 1 - label_at[distance]
            place = 6 + 2 * distance + core

            @pl.when(exists[distance])
            def _():
                arrived(label, place)

                @pl.when(through)
                def _():
                    send(4, label, place, 6 + 4 * distance + core, along(-distance))

                if turn == 0:

                    @pl.when(turns_corner[distance])
                    def _():
                        send(5, label, place, 1, corner)

                else:
                    send(distance % 4, None, place, place, sibling)

    def share(*distances):
        for distance in distances:
            place = 6 + 2 * distance + core

            @pl.when(exists[distance])
            def _():
                arrived(0, place)
                arrived(1, place)
                send(6 + distance // 2, None, place, place, sibling)

    def share_lone():
        @pl.when(lone)
        def _():
            arrived(across, 1)
            send(8, across, 1, 1, rung)

    def from_sibling(*distances):
        for distance in distances:
            take = copy_of(0, 2, (2, 7 + 2 * distance - core)).wait_recv
            when(exists[distance], take)

    def live_scale(place):
        live = partners[0, slot_of(place, core)] >= 0
        return jnp.where(live, jnp.float32((2 * BAND) ** -0.5), jnp.float32(0.0))

    def store(place, begin, end, tile):
        done[place - 4, begin:end] = tile

    def lag_other():
        lag_rows(window[other, mine, own, :], rows, turns, rotated, other)

    def group(first):
        correlate(rotated, window, first, 4, live_scale, store)

    def follow(first, second):
        pass_on(0, first, second)
        lag_other()
        pass_on(1, first, second)
        from_sibling(0, -1)
        group(4)
        share_lone()
        share(2 * first, 2 * second)
        from_sibling(1, 2)
        group(8)

    pl.when(spot == 0)(functools.partial(follow, 1, -1))
    pl.when(spot != 0)(functools.partial(follow, -1, 1))

    for place in range(1, 4):
        last_scales[place - 1] = jnp.full((8, 2 * CHB), live_scale(place), jnp.float32)
    from_sibling(-2)

    @pl.when(lone)
    def _():
        arrived(1 - across, 1)

    copy_of(0, 3, (0, 1)).wait_send()
    for distance in (1, -1):
        pl.when(exists[distance])(copy_of(distance % 4, 4, (0, 1)).wait_send)
        pl.when(exists[2 * distance])(copy_of(6 + distance, 2, (0, 1)).wait_send)
    pl.when(through)(copy_of(4, 4, (0, 1)).wait_send)
    pl.when(reaches_corner & exists[-1] & exists[1])(copy_of(5, 1, (0, 1)).wait_send)
    pl.when(lone)(copy_of(8, 1, (0, 1)).wait_send)


def finish_kernel(window, rotated, done, last_scales, out, last, out_sem):
    core = lax.axis_index("chan") % 2
    copies = []
    for k in range(IN_FIRST):
        copies.append(pltpu.make_async_copy(done.at[k], out.at[slot_of(4 + k, core)], out_sem.at[k]))
        copies[-1].start()

    def scale(place):
        return last_scales[place - 1, 0:1, :].reshape(1, 1, 2 * CHB)

    def store(place, begin, end, tile):
        last[place - 1, begin:end] = tile
        copies.append(
            pltpu.make_async_copy(
                last.at[place - 1, pl.ds(begin, end - begin)],
                out.at[slot_of(place, core), pl.ds(begin, end - begin)],
                out_sem.at[len(copies)],
            )
        )
        copies[-1].start()

    correlate(rotated, window, 1, 3, scale, store, PARTS)
    for copy in copies:
        copy.wait()


def local(traces, partners):
    transform, twiddle, turns = tables()
    in_hbm = pl.BlockSpec(memory_space=pltpu.HBM)
    in_vmem = pl.BlockSpec(memory_space=pltpu.VMEM)
    operands = [
        pltpu.with_memory_space_constraint(jnp.asarray(x), pltpu.HBM)
        for x in (traces, transform, twiddle, turns, partners)
    ]
    results = pl.pallas_call(
        gather_kernel,
        out_shape=(
            pltpu.VMEM((2, PLACES, CHB, 2 * BAND), jnp.bfloat16),
            pltpu.VMEM((2, LAGS * HALF, 2 * BAND), jnp.bfloat16),
            pltpu.VMEM((IN_FIRST, LAGS, PAIRS, 2 * CHB), jnp.float32),
            pltpu.VMEM((3, 8, 2 * CHB), jnp.float32),
        ),
        in_specs=[in_hbm] * 5,
        out_specs=(in_vmem,) * 4,
        scratch_shapes=[
            pltpu.VMEM((CHB, SAMPLES), jnp.bfloat16),
            pltpu.VMEM((2, COLS, 2 * BAND), jnp.bfloat16),
            pltpu.VMEM((2, FOLDS, BAND), jnp.float32),
            pltpu.VMEM((2, LAGS, BAND), jnp.float32),
            pltpu.VMEM((4, HALF, 128), jnp.float32),
            pltpu.SMEM((1, CAP), jnp.int32),
            pltpu.SemaphoreType.DMA((8,)),
            pltpu.SemaphoreType.DMA((9,)),
            pltpu.SemaphoreType.DMA((3, PLACES)),
        ],
        compiler_params=pltpu.CompilerParams(
            collective_id=0, has_side_effects=True, vmem_limit_bytes=40 * 2**20
        ),
        name="gather",
    )(*operands)
    out = pl.pallas_call(
        finish_kernel,
        out_shape=jax.ShapeDtypeStruct((CAP, LAGS, PAIRS, 2 * CHB), jnp.float32),
        in_specs=[in_vmem] * 4,
        out_specs=in_hbm,
        scratch_shapes=[
            pltpu.VMEM((3, LAGS, PAIRS, 2 * CHB), jnp.float32),
            pltpu.SemaphoreType.DMA((IN_FIRST + 3 * len(PARTS),)),
        ],
        compiler_params=pltpu.CompilerParams(vmem_limit_bytes=40 * 2**20),
        name="finish",
    )(*results)
    return out.reshape(1, CAP, LAGS, HALF * CHB)


def solution(mesh):
    placed = (P("seg", "chan", None), P("chan", None))
    return jax.shard_map(
        local, mesh=mesh, in_specs=placed, out_specs=P("chan", None, None, "seg"), check_vma=False
    )
```

```python
import functools
import math

import jax
import jax.numpy as jnp
import numpy as np
from jax import lax
from jax.experimental import pallas as pl
from jax.experimental.pallas import tpu as pltpu
from jax.sharding import PartitionSpec as P

CHB = 64
SAMPLES = 4096
BAND = 256
BAND_LO = 16
LAGS = 65
CAP = 11
COLS = 256
FOLDS = SAMPLES // COLS
PLACES = 12
IN_FIRST = 8
FULL_TURN = 2.0 * math.pi
WATER_LEVEL = 0.5
EPSILON = 1e-06
HALF = 32
PAIRS = HALF // 2
SHARED = 44
PARTS = ((0, 22), (22, 44), (44, 65))


def tables():
    bins = np.arange(BAND, dtype=np.int64) + BAND_LO
    fine = (np.arange(COLS, dtype=np.int64)[:, None] * bins[None, :]) % SAMPLES
    angle = fine * (FULL_TURN / SAMPLES)
    transform = np.concatenate([np.cos(angle), -np.sin(angle)], axis=1).astype(np.float32)
    high = transform.astype(jnp.bfloat16)
    low = (transform - high.astype(np.float32)).astype(jnp.bfloat16)
    coarse = (COLS * np.arange(FOLDS, dtype=np.int64)[:, None] * bins[None, :]) % SAMPLES
    turn = coarse * (FULL_TURN / SAMPLES)
    twiddle = np.stack([np.cos(turn), np.sin(turn)]).astype(np.float32)
    shifts = np.arange(LAGS, dtype=np.int64) - (LAGS - 1) // 2
    phase = ((shifts[:, None] * bins[None, :]) % SAMPLES) * (FULL_TURN / SAMPLES)
    turns = np.stack([np.cos(phase), np.sin(phase)]).astype(np.float32)
    return np.stack([high, low]), twiddle, turns


def spectra(samples, transform, twiddle):
    count = samples.shape[0]
    part = jnp.concatenate([samples[:, fold * COLS : (fold + 1) * COLS] for fold in range(FOLDS)], axis=0)
    partial = jnp.dot(part, transform[0], preferred_element_type=jnp.float32)
    partial = partial + jnp.dot(part, transform[1], preferred_element_type=jnp.float32)
    real, imag = partial[:count, :BAND], partial[:count, BAND:]
    for fold in range(1, FOLDS):
        re = partial[fold * count : (fold + 1) * count, :BAND]
        im = partial[fold * count : (fold + 1) * count, BAND:]
        cosine = twiddle[0, pl.ds(fold, 1), :]
        sine = twiddle[1, pl.ds(fold, 1), :]
        real = real + (re * cosine + im * sine)
        imag = imag + (im * cosine - re * sine)
    power = real * real + imag * imag
    level = jnp.sum(power, axis=-1, keepdims=True) * (1.0 / BAND)
    denom = jnp.sqrt(power + WATER_LEVEL * level + EPSILON)
    return jnp.concatenate([real / denom, imag / denom], axis=-1).astype(jnp.bfloat16)


def lag_rows(white, rows, turns, rotated, segment):
    for part in range(4):
        rows[part] = white[:, part * 128 : (part + 1) * 128].astype(jnp.float32)
    split = jnp.concatenate(
        [
            jnp.concatenate([rows[part, pl.ds(odd, PAIRS, stride=2), :] for part in range(4)], axis=1)
            for odd in range(2)
        ],
        axis=0,
    )
    re, im = split[:, :BAND], split[:, BAND:]

    @pl.loop(0, LAGS // 5)
    def _(step):
        for inner in range(5):
            lag = step * 5 + inner
            cosine = turns[0, pl.ds(lag, 1), :]
            sine = turns[1, pl.ds(lag, 1), :]
            at = pl.ds(pl.multiple_of(lag * HALF, HALF), HALF)
            rotated[segment, at, :BAND] = (re * cosine - im * sine).astype(jnp.bfloat16)
            rotated[segment, at, BAND:] = (re * sine + im * cosine).astype(jnp.bfloat16)


def correlate(rotated, window, first, count, scale_of, store, parts=((0, LAGS),)):
    right = jnp.concatenate(
        [window[seg, first : first + count].reshape(count * CHB, 2 * BAND) for seg in range(2)], axis=1
    )
    for begin, end in parts:
        lags = end - begin
        left = jnp.concatenate([rotated[seg, begin * HALF : end * HALF, :] for seg in range(2)], axis=1)
        product = lax.dot_general(left, right, (((1,), (1,)), ((), ())), preferred_element_type=jnp.float32)
        product = product.reshape(lags, 2, PAIRS, count * CHB)
        low_half = lax.broadcasted_iota(jnp.int32, (lags, PAIRS, 2 * CHB), 2) < CHB
        for k in range(0, count, 2):
            width = min(2, count - k) * CHB
            even = product[:, 0, :, k * CHB : k * CHB + width]
            odd = product[:, 1, :, k * CHB : k * CHB + width]
            if width < 2 * CHB:
                store(first + k, begin, end, jnp.concatenate([even, odd], axis=2) * scale_of(first + k))
            else:
                here = jnp.where(low_half, even, pltpu.roll(odd, CHB, 2))
                there = jnp.where(low_half, pltpu.roll(even, CHB, 2), odd)
                store(first + k, begin, end, here * scale_of(first + k))
                store(first + k + 1, begin, end, there * scale_of(first + k + 1))


def slot_of(place, core):
    if isinstance(place, int) and place == 1:
        return 10 * core
    return place - 1 - core


def gather_kernel(
    traces, transform_in, twiddle_in, turns_in, partners_in,
    window, rotated, done, last_scales,
    samples, transform, twiddle, turns, rows, partners, in_sem, send_sem, recv_sem,
):
    seg = lax.axis_index("seg")
    chan = lax.axis_index("chan")
    core = chan % 2
    chip = chan // 2
    spot = chip % 8
    other = 1 - seg
    total = lax.axis_size("chan")
    chips = total // 2
    mine = 6 + core

    tables_in = [
        pltpu.make_async_copy(transform_in, transform, in_sem.at[4]),
        pltpu.make_async_copy(twiddle_in, twiddle, in_sem.at[5]),
    ]
    loads = [
        pltpu.make_async_copy(
            traces.at[0, pl.ds(half * HALF, HALF), :], samples.at[pl.ds(half * HALF, HALF), :], in_sem.at[half]
        )
        for half in range(2)
    ]
    later = [
        pltpu.make_async_copy(turns_in, turns, in_sem.at[6]),
        pltpu.make_async_copy(partners_in, partners, in_sem.at[7]),
    ]
    for load in tables_in + loads + later:
        load.start()

    def there_is(distance):
        return (chip + distance >= 0) & (chip + distance < chips)

    def segment_at(distance):
        crossed = (spot + distance < 0) | (spot + distance > 7)
        return jnp.where(crossed, other, seg)

    outward = 2 * core - 1
    exists = {distance: there_is(distance) for distance in (-2, -1, 1, 2)}
    exists[0] = None
    lone = there_is(3 * outward)
    reaches_corner = there_is(2 * outward)
    turns_corner = {distance: exists[distance] & reaches_corner & (outward == -distance) for distance in (-1, 1)}
    through = exists[1] & exists[-1]
    label_at = {distance: segment_at(distance) for distance in (-2, -1, 1, 2)}
    across = segment_at(3 * outward)

    def along(distance, cross=False):
        label = label_at[distance]
        return {"seg": 1 - label if cross else label, "chan": (chan + total + 2 * distance) % total}

    rung = {"seg": other, "chan": chan}
    sibling = {"seg": seg, "chan": chan + 1 - 2 * core}
    corner = {"seg": segment_at(2 * outward), "chan": (chan + total + 3 * outward) % total}

    def when(valid, act):
        if valid is None:
            act()
        else:
            pl.when(valid)(act)

    barrier = pltpu.get_barrier_semaphore()

    def greet(device):
        pl.semaphore_signal(barrier, inc=1, device_id=device, device_id_type=pl.DeviceIdType.MESH)

    greet(rung)
    greet(sibling)
    greeted = jnp.int32(2)
    for distance in (1, -1):

        @pl.when(exists[distance])
        def _():
            greet(along(distance))
            greet(along(distance, True))

        greeted = greeted + jnp.where(exists[distance], 2, 0)
    pl.when(reaches_corner)(lambda: greet(corner))
    greeted = greeted + jnp.where(reaches_corner, 1, 0)

    def send(key, label, source, target, device):
        both = label is None
        copy = pltpu.make_async_remote_copy(
            src_ref=window.at[:, source] if both else window.at[label, source],
            dst_ref=window.at[:, target] if both else window.at[label, target],
            send_sem=send_sem.at[key],
            recv_sem=recv_sem.at[2 if both else label, target],
            device_id=device,
            device_id_type=pl.DeviceIdType.MESH,
        )
        copy.start()

    def copy_of(number, blocks, place):
        return pltpu.make_async_remote_copy(
            src_ref=window.at[0, 0:blocks],
            dst_ref=window.at[0, 0:blocks],
            send_sem=send_sem.at[number],
            recv_sem=recv_sem.at[place],
            device_id=rung,
            device_id_type=pl.DeviceIdType.MESH,
        )

    def arrived(label, place):
        copy_of(0, 1, (label, place)).wait_recv()

    def own_to(distance, cross):
        send(distance % 4, seg, mine, 6 - 2 * distance + core, along(distance, cross))

    def own_out(cross):
        for distance in (1, -1):
            pl.when(exists[distance])(functools.partial(own_to, distance, cross))

    for load in tables_in + loads:
        load.wait()
    window[seg, mine] = spectra(samples[...], transform, twiddle)
    pl.semaphore_wait(barrier, greeted)
    own_out(False)
    own_out(True)
    send(0, seg, mine, mine, rung)

    for distance in (-2, -1, 1, 2):

        @pl.when(jnp.logical_not(exists[distance]))
        def _():
            window[:, 6 + 2 * distance : 8 + 2 * distance] = jnp.zeros((2, 2, CHB, 2 * BAND), jnp.bfloat16)

    @pl.when(jnp.logical_not(lone))
    def _():
        window[:, 1] = jnp.zeros((2, CHB, 2 * BAND), jnp.bfloat16)

    for load in later:
        load.wait()
    own = pl.ds(pl.multiple_of(seg * HALF, HALF), HALF)
    lag_rows(window[seg, mine, own, :], rows, turns, rotated, seg)


    def pass_on(turn, *distances):
        for distance in distances:
            label = label_at[distance] if turn == 0 else 1 - label_at[distance]
            place = 6 + 2 * distance + core

            @pl.when(exists[distance])
            def _():
                arrived(label, place)

                @pl.when(through)
                def _():
                    send(4, label, place, 6 + 4 * distance + core, along(-distance))

                if turn == 0:

                    @pl.when(turns_corner[distance])
                    def _():
                        send(5, label, place, 1, corner)

                else:
                    send(distance % 4, None, place, place, sibling)

    def share(*distances):
        for distance in distances:
            place = 6 + 2 * distance + core

            @pl.when(exists[distance])
            def _():
                arrived(0, place)
                arrived(1, place)
                send(6 + distance // 2, None, place, place, sibling)

    def share_lone():
        @pl.when(lone)
        def _():
            arrived(across, 1)
            send(8, across, 1, 1, rung)

    def from_sibling(*distances):
        for distance in distances:
            take = copy_of(0, 2, (2, 7 + 2 * distance - core)).wait_recv
            when(exists[distance], take)

    def live_scale(place):
        live = partners[0, slot_of(place, core)] >= 0
        return jnp.where(live, jnp.float32((2 * BAND) ** -0.5), jnp.float32(0.0))

    def store(place, begin, end, tile):
        done[place - 4, begin:end] = tile

    def lag_other():
        arrived(other, mine)
        send(0, None, mine, mine, sibling)
        lag_rows(window[other, mine, own, :], rows, turns, rotated, other)

    def group(first, lags=LAGS):
        correlate(rotated, window, first, 4, live_scale, store, ((0, lags),))

    def follow(first, second):
        pass_on(0, first, second)
        pass_on(1, first, second)
        lag_other()
        from_sibling(0, -1)
        group(4)
        share_lone()
        share(2 * first, 2 * second)
        from_sibling(1, 2)
        group(8, SHARED)

    pl.when(spot == 0)(functools.partial(follow, 1, -1))
    pl.when(spot != 0)(functools.partial(follow, -1, 1))

    for place in (1, 2, 3, 8, 9, 10, 11):
        last_scales[place] = jnp.full((8, 2 * CHB), live_scale(place), jnp.float32)
    from_sibling(-2)

    @pl.when(lone)
    def _():
        arrived(1 - across, 1)

    copy_of(0, 3, (0, 1)).wait_send()
    for distance in (1, -1):
        pl.when(exists[distance])(copy_of(distance % 4, 4, (0, 1)).wait_send)
        pl.when(exists[2 * distance])(copy_of(6 + distance, 2, (0, 1)).wait_send)
    pl.when(through)(copy_of(4, 4, (0, 1)).wait_send)
    pl.when(reaches_corner & exists[-1] & exists[1])(copy_of(5, 1, (0, 1)).wait_send)
    pl.when(lone)(copy_of(8, 1, (0, 1)).wait_send)


def finish_kernel(window, rotated, done, last_scales, out, last, out_sem):
    core = lax.axis_index("chan") % 2
    copies = []
    for k in range(IN_FIRST):
        lags = pl.ds(0, LAGS if k < 4 else SHARED)
        copies.append(
            pltpu.make_async_copy(done.at[k, lags], out.at[slot_of(4 + k, core), lags], out_sem.at[k])
        )
        copies[-1].start()

    def scale(place):
        return last_scales[place, 0:1, :].reshape(1, 1, 2 * CHB)

    def store(place, begin, end, tile):
        row = place - 1 if place < 4 else place - 5
        last[row, begin:end] = tile
        copies.append(
            pltpu.make_async_copy(
                last.at[row, pl.ds(begin, end - begin)],
                out.at[slot_of(place, core), pl.ds(begin, end - begin)],
                out_sem.at[len(copies)],
            )
        )
        copies[-1].start()

    correlate(rotated, window, 8, 4, scale, store, ((SHARED, LAGS),))
    correlate(rotated, window, 1, 3, scale, store, PARTS)
    for copy in copies:
        copy.wait()


def local(traces, partners):
    transform, twiddle, turns = tables()
    in_hbm = pl.BlockSpec(memory_space=pltpu.HBM)
    in_vmem = pl.BlockSpec(memory_space=pltpu.VMEM)
    operands = [
        pltpu.with_memory_space_constraint(jnp.asarray(x), pltpu.HBM)
        for x in (traces, transform, twiddle, turns, partners)
    ]
    results = pl.pallas_call(
        gather_kernel,
        out_shape=(
            pltpu.VMEM((2, PLACES, CHB, 2 * BAND), jnp.bfloat16),
            pltpu.VMEM((2, LAGS * HALF, 2 * BAND), jnp.bfloat16),
            pltpu.VMEM((IN_FIRST, LAGS, PAIRS, 2 * CHB), jnp.float32),
            pltpu.VMEM((PLACES, 8, 2 * CHB), jnp.float32),
        ),
        in_specs=[in_hbm] * 5,
        out_specs=(in_vmem,) * 4,
        scratch_shapes=[
            pltpu.VMEM((CHB, SAMPLES), jnp.bfloat16),
            pltpu.VMEM((2, COLS, 2 * BAND), jnp.bfloat16),
            pltpu.VMEM((2, FOLDS, BAND), jnp.float32),
            pltpu.VMEM((2, LAGS, BAND), jnp.float32),
            pltpu.VMEM((4, HALF, 128), jnp.float32),
            pltpu.SMEM((1, CAP), jnp.int32),
            pltpu.SemaphoreType.DMA((8,)),
            pltpu.SemaphoreType.DMA((9,)),
            pltpu.SemaphoreType.DMA((3, PLACES)),
        ],
        compiler_params=pltpu.CompilerParams(
            collective_id=0, has_side_effects=True, vmem_limit_bytes=40 * 2**20
        ),
        name="gather",
    )(*operands)
    out = pl.pallas_call(
        finish_kernel,
        out_shape=jax.ShapeDtypeStruct((CAP, LAGS, PAIRS, 2 * CHB), jnp.float32),
        in_specs=[in_vmem] * 4,
        out_specs=in_hbm,
        scratch_shapes=[
            pltpu.VMEM((7, LAGS, PAIRS, 2 * CHB), jnp.float32),
            pltpu.SemaphoreType.DMA((IN_FIRST + 4 + 3 * len(PARTS),)),
        ],
        compiler_params=pltpu.CompilerParams(vmem_limit_bytes=40 * 2**20),
        name="finish",
    )(*results)
    return out.reshape(1, CAP, LAGS, HALF * CHB)


def solution(mesh):
    placed = (P("seg", "chan", None), P("chan", None))
    return jax.shard_map(
        local, mesh=mesh, in_specs=placed, out_specs=P("chan", None, None, "seg"), check_vma=False
    )
```

```python
import functools
import math

import jax
import jax.numpy as jnp
import numpy as np
from jax import lax
from jax.experimental import pallas as pl
from jax.experimental.pallas import tpu as pltpu
from jax.sharding import PartitionSpec as P

CHB = 64
SAMPLES = 4096
BAND = 256
BAND_LO = 16
LAGS = 65
CAP = 11
COLS = 256
FOLDS = SAMPLES // COLS
PLACES = 12
IN_FIRST = 8
FULL_TURN = 2.0 * math.pi
WATER_LEVEL = 0.5
EPSILON = 1e-06
HALF = 32
PAIRS = HALF // 2
SHARED = 33
PARTS = ((0, 22), (22, 44), (44, 65))


def tables():
    bins = np.arange(BAND, dtype=np.int64) + BAND_LO
    fine = (np.arange(COLS, dtype=np.int64)[:, None] * bins[None, :]) % SAMPLES
    angle = fine * (FULL_TURN / SAMPLES)
    transform = np.concatenate([np.cos(angle), -np.sin(angle)], axis=1).astype(np.float32)
    high = transform.astype(jnp.bfloat16)
    low = (transform - high.astype(np.float32)).astype(jnp.bfloat16)
    coarse = (COLS * np.arange(FOLDS, dtype=np.int64)[:, None] * bins[None, :]) % SAMPLES
    turn = coarse * (FULL_TURN / SAMPLES)
    twiddle = np.stack([np.cos(turn), np.sin(turn)]).astype(np.float32)
    shifts = np.arange(LAGS, dtype=np.int64) - (LAGS - 1) // 2
    phase = ((shifts[:, None] * bins[None, :]) % SAMPLES) * (FULL_TURN / SAMPLES)
    turns = np.stack([np.cos(phase), np.sin(phase)]).astype(np.float32)
    return np.stack([high, low]), twiddle, turns


def spectra(samples, transform, twiddle):
    count = samples.shape[0]
    part = jnp.concatenate([samples[:, fold * COLS : (fold + 1) * COLS] for fold in range(FOLDS)], axis=0)
    partial = jnp.dot(part, transform[0], preferred_element_type=jnp.float32)
    partial = partial + jnp.dot(part, transform[1], preferred_element_type=jnp.float32)
    real, imag = partial[:count, :BAND], partial[:count, BAND:]
    for fold in range(1, FOLDS):
        re = partial[fold * count : (fold + 1) * count, :BAND]
        im = partial[fold * count : (fold + 1) * count, BAND:]
        cosine = twiddle[0, pl.ds(fold, 1), :]
        sine = twiddle[1, pl.ds(fold, 1), :]
        real = real + (re * cosine + im * sine)
        imag = imag + (im * cosine - re * sine)
    power = real * real + imag * imag
    level = jnp.sum(power, axis=-1, keepdims=True) * (1.0 / BAND)
    denom = jnp.sqrt(power + WATER_LEVEL * level + EPSILON)
    return jnp.concatenate([real / denom, imag / denom], axis=-1).astype(jnp.bfloat16)


def lag_rows(white, rows, turns, rotated, segment):
    for part in range(4):
        rows[part] = white[:, part * 128 : (part + 1) * 128].astype(jnp.float32)
    split = jnp.concatenate(
        [
            jnp.concatenate([rows[part, pl.ds(odd, PAIRS, stride=2), :] for part in range(4)], axis=1)
            for odd in range(2)
        ],
        axis=0,
    )
    re, im = split[:, :BAND], split[:, BAND:]

    @pl.loop(0, LAGS // 5)
    def _(step):
        for inner in range(5):
            lag = step * 5 + inner
            cosine = turns[0, pl.ds(lag, 1), :]
            sine = turns[1, pl.ds(lag, 1), :]
            at = pl.ds(pl.multiple_of(lag * HALF, HALF), HALF)
            rotated[segment, at, :BAND] = (re * cosine - im * sine).astype(jnp.bfloat16)
            rotated[segment, at, BAND:] = (re * sine + im * cosine).astype(jnp.bfloat16)


def correlate(rotated, window, first, count, scale_of, store, parts=((0, LAGS),)):
    right = jnp.concatenate(
        [window[seg, first : first + count].reshape(count * CHB, 2 * BAND) for seg in range(2)], axis=1
    )
    for begin, end in parts:
        lags = end - begin
        left = jnp.concatenate([rotated[seg, begin * HALF : end * HALF, :] for seg in range(2)], axis=1)
        product = lax.dot_general(left, right, (((1,), (1,)), ((), ())), preferred_element_type=jnp.float32)
        product = product.reshape(lags, 2, PAIRS, count * CHB)
        low_half = lax.broadcasted_iota(jnp.int32, (lags, PAIRS, 2 * CHB), 2) < CHB
        for k in range(0, count, 2):
            width = min(2, count - k) * CHB
            even = product[:, 0, :, k * CHB : k * CHB + width]
            odd = product[:, 1, :, k * CHB : k * CHB + width]
            if width < 2 * CHB:
                store(first + k, begin, end, jnp.concatenate([even, odd], axis=2) * scale_of(first + k))
            else:
                here = jnp.where(low_half, even, pltpu.roll(odd, CHB, 2))
                there = jnp.where(low_half, pltpu.roll(even, CHB, 2), odd)
                store(first + k, begin, end, here * scale_of(first + k))
                store(first + k + 1, begin, end, there * scale_of(first + k + 1))


def slot_of(place, core):
    if isinstance(place, int) and place == 1:
        return 10 * core
    return place - 1 - core


def gather_kernel(
    traces, transform_in, twiddle_in, turns_in, partners_in,
    window, rotated, done, last_scales,
    samples, transform, twiddle, turns, rows, partners, in_sem, send_sem, recv_sem,
):
    seg = lax.axis_index("seg")
    chan = lax.axis_index("chan")
    core = chan % 2
    chip = chan // 2
    spot = chip % 8
    other = 1 - seg
    total = lax.axis_size("chan")
    chips = total // 2
    mine = 6 + core

    tables_in = [
        pltpu.make_async_copy(transform_in, transform, in_sem.at[4]),
        pltpu.make_async_copy(twiddle_in, twiddle, in_sem.at[5]),
    ]
    loads = [
        pltpu.make_async_copy(
            traces.at[0, pl.ds(half * HALF, HALF), :], samples.at[pl.ds(half * HALF, HALF), :], in_sem.at[half]
        )
        for half in range(2)
    ]
    later = [
        pltpu.make_async_copy(turns_in, turns, in_sem.at[6]),
        pltpu.make_async_copy(partners_in, partners, in_sem.at[7]),
    ]
    for load in tables_in + loads + later:
        load.start()

    def there_is(distance):
        return (chip + distance >= 0) & (chip + distance < chips)

    def segment_at(distance):
        crossed = (spot + distance < 0) | (spot + distance > 7)
        return jnp.where(crossed, other, seg)

    outward = 2 * core - 1
    exists = {distance: there_is(distance) for distance in (-2, -1, 1, 2)}
    exists[0] = None
    lone = there_is(3 * outward)
    reaches_corner = there_is(2 * outward)
    turns_corner = {distance: exists[distance] & reaches_corner & (outward == -distance) for distance in (-1, 1)}
    through = exists[1] & exists[-1]
    label_at = {distance: segment_at(distance) for distance in (-2, -1, 1, 2)}
    across = segment_at(3 * outward)

    def along(distance, cross=False):
        label = label_at[distance]
        return {"seg": 1 - label if cross else label, "chan": (chan + total + 2 * distance) % total}

    rung = {"seg": other, "chan": chan}
    sibling = {"seg": seg, "chan": chan + 1 - 2 * core}
    corner = {"seg": segment_at(2 * outward), "chan": (chan + total + 3 * outward) % total}

    def when(valid, act):
        if valid is None:
            act()
        else:
            pl.when(valid)(act)

    barrier = pltpu.get_barrier_semaphore()

    def greet(device):
        pl.semaphore_signal(barrier, inc=1, device_id=device, device_id_type=pl.DeviceIdType.MESH)

    greet(rung)
    greet(sibling)
    greeted = jnp.int32(2)
    for distance in (1, -1):

        @pl.when(exists[distance])
        def _():
            greet(along(distance))
            greet(along(distance, True))

        greeted = greeted + jnp.where(exists[distance], 2, 0)
    pl.when(reaches_corner)(lambda: greet(corner))
    greeted = greeted + jnp.where(reaches_corner, 1, 0)

    def send(key, label, source, target, device):
        both = label is None
        copy = pltpu.make_async_remote_copy(
            src_ref=window.at[:, source] if both else window.at[label, source],
            dst_ref=window.at[:, target] if both else window.at[label, target],
            send_sem=send_sem.at[key],
            recv_sem=recv_sem.at[2 if both else label, target],
            device_id=device,
            device_id_type=pl.DeviceIdType.MESH,
        )
        copy.start()

    def copy_of(number, blocks, place):
        return pltpu.make_async_remote_copy(
            src_ref=window.at[0, 0:blocks],
            dst_ref=window.at[0, 0:blocks],
            send_sem=send_sem.at[number],
            recv_sem=recv_sem.at[place],
            device_id=rung,
            device_id_type=pl.DeviceIdType.MESH,
        )

    def arrived(label, place):
        copy_of(0, 1, (label, place)).wait_recv()

    def own_to(distance, cross):
        send(distance % 4, seg, mine, 6 - 2 * distance + core, along(distance, cross))

    def own_out(cross):
        for distance in (1, -1):
            pl.when(exists[distance])(functools.partial(own_to, distance, cross))

    for load in tables_in + loads:
        load.wait()
    window[seg, mine] = spectra(samples[...], transform, twiddle)
    pl.semaphore_wait(barrier, greeted)
    own_out(False)
    own_out(True)
    send(0, seg, mine, mine, rung)

    for distance in (-2, -1, 1, 2):

        @pl.when(jnp.logical_not(exists[distance]))
        def _():
            window[:, 6 + 2 * distance : 8 + 2 * distance] = jnp.zeros((2, 2, CHB, 2 * BAND), jnp.bfloat16)

    @pl.when(jnp.logical_not(lone))
    def _():
        window[:, 1] = jnp.zeros((2, CHB, 2 * BAND), jnp.bfloat16)

    for load in later:
        load.wait()
    own = pl.ds(pl.multiple_of(seg * HALF, HALF), HALF)
    lag_rows(window[seg, mine, own, :], rows, turns, rotated, seg)


    def pass_on(turn, *distances):
        for distance in distances:
            label = label_at[distance] if turn == 0 else 1 - label_at[distance]
            place = 6 + 2 * distance + core

            @pl.when(exists[distance])
            def _():
                arrived(label, place)

                @pl.when(through)
                def _():
                    send(4, label, place, 6 + 4 * distance + core, along(-distance))

                if turn == 0:

                    @pl.when(turns_corner[distance])
                    def _():
                        send(5, label, place, 1, corner)

                else:
                    send(distance % 4, None, place, place, sibling)

    def share(*distances):
        for distance in distances:
            place = 6 + 2 * distance + core

            @pl.when(exists[distance])
            def _():
                arrived(0, place)
                arrived(1, place)
                send(6 + distance // 2, None, place, place, sibling)

    def share_lone():
        @pl.when(lone)
        def _():
            arrived(across, 1)
            send(8, across, 1, 1, rung)

    def from_sibling(*distances):
        for distance in distances:
            take = copy_of(0, 2, (2, 7 + 2 * distance - core)).wait_recv
            when(exists[distance], take)

    def live_scale(place):
        live = partners[0, slot_of(place, core)] >= 0
        return jnp.where(live, jnp.float32((2 * BAND) ** -0.5), jnp.float32(0.0))

    def store(place, begin, end, tile):
        done[place - 4, begin:end] = tile

    def lag_other():
        arrived(other, mine)
        send(0, None, mine, mine, sibling)
        lag_rows(window[other, mine, own, :], rows, turns, rotated, other)

    def group(first, lags=LAGS):
        correlate(rotated, window, first, 4, live_scale, store, ((0, lags),))

    def follow(first, second):
        pass_on(0, first, second)
        pass_on(1, first, second)
        lag_other()
        from_sibling(0, -1)
        group(4)
        share_lone()
        share(2 * first, 2 * second)
        from_sibling(1, 2)
        group(8, SHARED)

    pl.when(spot == 0)(functools.partial(follow, 1, -1))
    pl.when(spot != 0)(functools.partial(follow, -1, 1))

    for place in (1, 2, 3, 8, 9, 10, 11):
        last_scales[place] = jnp.full((8, 2 * CHB), live_scale(place), jnp.float32)
    from_sibling(-2)

    @pl.when(lone)
    def _():
        arrived(1 - across, 1)

    copy_of(0, 3, (0, 1)).wait_send()
    for distance in (1, -1):
        pl.when(exists[distance])(copy_of(distance % 4, 4, (0, 1)).wait_send)
        pl.when(exists[2 * distance])(copy_of(6 + distance, 2, (0, 1)).wait_send)
    pl.when(through)(copy_of(4, 4, (0, 1)).wait_send)
    pl.when(reaches_corner & exists[-1] & exists[1])(copy_of(5, 1, (0, 1)).wait_send)
    pl.when(lone)(copy_of(8, 1, (0, 1)).wait_send)


def finish_kernel(window, rotated, done, last_scales, out, last, out_sem):
    core = lax.axis_index("chan") % 2
    copies = []
    for k in range(IN_FIRST):
        lags = pl.ds(0, LAGS if k < 4 else SHARED)
        copies.append(
            pltpu.make_async_copy(done.at[k, lags], out.at[slot_of(4 + k, core), lags], out_sem.at[k])
        )
        copies[-1].start()

    def scale(place):
        return last_scales[place, 0:1, :].reshape(1, 1, 2 * CHB)

    def store(place, begin, end, tile):
        row = place - 1 if place < 4 else place - 5
        last[row, begin:end] = tile
        copies.append(
            pltpu.make_async_copy(
                last.at[row, pl.ds(begin, end - begin)],
                out.at[slot_of(place, core), pl.ds(begin, end - begin)],
                out_sem.at[len(copies)],
            )
        )
        copies[-1].start()

    correlate(rotated, window, 8, 4, scale, store, ((SHARED, LAGS),))
    correlate(rotated, window, 1, 3, scale, store, PARTS)
    for copy in copies:
        copy.wait()


def local(traces, partners):
    transform, twiddle, turns = tables()
    in_hbm = pl.BlockSpec(memory_space=pltpu.HBM)
    in_vmem = pl.BlockSpec(memory_space=pltpu.VMEM)
    operands = [
        pltpu.with_memory_space_constraint(jnp.asarray(x), pltpu.HBM)
        for x in (traces, transform, twiddle, turns, partners)
    ]
    results = pl.pallas_call(
        gather_kernel,
        out_shape=(
            pltpu.VMEM((2, PLACES, CHB, 2 * BAND), jnp.bfloat16),
            pltpu.VMEM((2, LAGS * HALF, 2 * BAND), jnp.bfloat16),
            pltpu.VMEM((IN_FIRST, LAGS, PAIRS, 2 * CHB), jnp.float32),
            pltpu.VMEM((PLACES, 8, 2 * CHB), jnp.float32),
        ),
        in_specs=[in_hbm] * 5,
        out_specs=(in_vmem,) * 4,
        scratch_shapes=[
            pltpu.VMEM((CHB, SAMPLES), jnp.bfloat16),
            pltpu.VMEM((2, COLS, 2 * BAND), jnp.bfloat16),
            pltpu.VMEM((2, FOLDS, BAND), jnp.float32),
            pltpu.VMEM((2, LAGS, BAND), jnp.float32),
            pltpu.VMEM((4, HALF, 128), jnp.float32),
            pltpu.SMEM((1, CAP), jnp.int32),
            pltpu.SemaphoreType.DMA((8,)),
            pltpu.SemaphoreType.DMA((9,)),
            pltpu.SemaphoreType.DMA((3, PLACES)),
        ],
        compiler_params=pltpu.CompilerParams(
            collective_id=0, has_side_effects=True, vmem_limit_bytes=40 * 2**20
        ),
        name="gather",
    )(*operands)
    out = pl.pallas_call(
        finish_kernel,
        out_shape=jax.ShapeDtypeStruct((CAP, LAGS, PAIRS, 2 * CHB), jnp.float32),
        in_specs=[in_vmem] * 4,
        out_specs=in_hbm,
        scratch_shapes=[
            pltpu.VMEM((7, LAGS, PAIRS, 2 * CHB), jnp.float32),
            pltpu.SemaphoreType.DMA((IN_FIRST + 4 + 3 * len(PARTS),)),
        ],
        compiler_params=pltpu.CompilerParams(vmem_limit_bytes=40 * 2**20),
        name="finish",
    )(*results)
    return out.reshape(1, CAP, LAGS, HALF * CHB)


def solution(mesh):
    placed = (P("seg", "chan", None), P("chan", None))
    return jax.shard_map(
        local, mesh=mesh, in_specs=placed, out_specs=P("chan", None, None, "seg"), check_vma=False
    )
```
